32 devices in a mesh: groups: 2 (over y), ep: 16 (over z, x, core).
Axes of the slice: x: 2, y: 2, z: 4, core: 2. Of those that a mesh axis runs over, the one named last changes fastest.
Arguments:
- hidden: bfloat16 [64, 7168], P(('groups', 'ep')), parts along dimension 0, may hold values from -6 to 6
- queries: bfloat16 [64, 128, 576], P(('groups', 'ep')), parts along dimension 0, may hold values from -40 to 40
- latent_cache: bfloat16 [64, 2048, 576], P(('groups', 'ep')), parts along dimension 0, may hold values from -8 to 8
- cache_lengths: int32 [64], P(('groups', 'ep')), parts along dimension 0, may hold values from 2 to 2048, as said below
- value_up: bfloat16 [128, 512, 128], P('ep'), may hold values from -0.25 to 0.25
- out_proj: bfloat16 [16384, 7168], P('ep'), may hold values from -0.046875 to 0.046875
- norm_gain: float32 [7168], replicated, may hold values from 0.1 to 1.9
- expert_ids: int32 [64, 8], P(('groups', 'ep')), parts along dimension 0, may hold values from 0 to 15, all different within a row; in each aligned block of 2 rows (0 to 1, 2 to 3, ...) at most 2 rows name the same one
- gate_weights: float32 [64, 8], P(('groups', 'ep')), parts along dimension 0, may hold values from 0.05 to 0.5
- gate_proj: bfloat16 [16, 7168, 1024], P('ep'), may hold values from -0.0625 to 0.0625
- up_proj: bfloat16 [16, 7168, 1024], P('ep'), may hold values from -0.0625 to 0.0625
- down_proj: bfloat16 [16, 1024, 7168], P('ep'), may hold values from -0.1875 to 0.1875
Outputs:
- layer_out: bfloat16 [64, 7168], P(('groups', 'ep')), parts along dimension 0
The draws below stay inside these ranges and needn't reach their ends.
There are 2 independent parts, one for each index of `groups`. The reference program is written for one: setup_inputs(seed, part) draws one part's arguments, and reference() takes and returns one part's arrays. A program takes and returns all parts, laid end to end along the dimension named above; an argument that names none is the same for every part. Nothing has to cross between parts.
Inputs may be any that keep to these rules, and one draw needn't show every extreme that they name: `cache_lengths`: some row of each draw has exactly 2048 live positions and some row exactly 2. `expert_ids`: each row names 8 different experts. The 2 rows of one device name any one expert at most 2 times, so a device sends each expert at most 2 rows; some device of every draw reaches that.
All inputs are finite; a program needn't handle non-finite values.
Results may differ from the reference program's by a relative error of at most 0.0095.
Values may be sent and summed in bfloat16 or wider, within the bound.
A program may use at most 128 MiB of HBM per device.

```python
import math
import jax
import jax.numpy as jnp
import numpy as np
from jax import lax

D = 7168
FF = 1024
HEADS = 128
LAT = 512
VDIM = 128
EXPERTS = 16
TOPK = 8
ROWS_DEV = 2
CTX = 2048
KDIM = 576
ROWS = 32
SPLIT = 1
DSL = 7168


def cache_front(key):
    lead_keys = jax.random.normal(jax.random.fold_in(key, 11), (ROWS, 1, KDIM), jnp.float32)
    offset_noise = 0.3 * jax.random.normal(jax.random.fold_in(key, 12), (ROWS, 1, KDIM), jnp.float32)
    return (lead_keys, lead_keys + offset_noise)


def draw_latent_cache(key, part):
    lead_keys, near_keys = cache_front(key)
    remaining = jax.random.normal(jax.random.fold_in(key, 13), (ROWS, CTX - 2, KDIM), jnp.float32)
    return jnp.concatenate([lead_keys, near_keys, remaining], axis=1).astype(jnp.bfloat16)


def draw_queries(key, part):
    drawn_query = jax.random.normal(jax.random.fold_in(key, 21), (ROWS, HEADS, KDIM), jnp.float32)
    return drawn_query.astype(jnp.bfloat16)


def draw_cache_lengths(key, part):
    lengths = jax.random.randint(jax.random.fold_in(key, 31), (ROWS,), 2, CTX + 1, jnp.int32)
    long_row = jax.random.randint(jax.random.fold_in(key, 32), (), 0, ROWS, jnp.int32)
    step_over = jax.random.randint(jax.random.fold_in(key, 33), (), 0, ROWS - 1, jnp.int32)
    short_row = (long_row + 1 + step_over) % ROWS
    return lengths.at[long_row].set(CTX).at[short_row].set(2)


def block_levels(stream_key, extent, split, smallest, high):
    def one(axis_at, blocks):
        heights = jax.random.uniform(jax.random.fold_in(jax.random.fold_in(stream_key, 6), axis_at), (blocks,), jnp.float32, smallest / len(split), high / len(split))
        return jnp.repeat(jnp.exp(heights), extent[axis_at] // blocks).reshape((-1,) + (1,) * (len(extent) - axis_at - 1))

    level = one(*split[0])
    for cut in split[1:]:
        level = level * one(*cut)
    return level


def deal_out(rng, own, number, rows, count, top, limit, lean):
    sequence = jax.random.permutation(rng, count)
    crowded, common = shares(count, rows * top, limit, lean, True), shares(count, rows * top, limit, lean, False)
    places = jnp.arange(count)

    def named(sizes, turn):
        used = int((sizes > 0).sum())
        fixed = max(1, used // 4)
        shifted = fixed + (places - fixed + turn * (used - fixed)) % max(1, count - fixed)
        return jnp.zeros((count,), jnp.int32).at[sequence[jnp.where(places < fixed, places, shifted)]].set(jnp.asarray(sizes, jnp.int32))

    sizes = jnp.where(number % 4 == 0, named(crowded, number // 4), named(common, number - number // 4 - 1))
    mixed = jax.random.permutation(jax.random.fold_in(own, 3), count)
    giver, taker = mixed[0:count // 2 * 2:2], mixed[1:count // 2 * 2:2]
    slack = jnp.minimum(sizes[giver] - 1, limit - sizes[taker]) // 2
    slack = jnp.where((giver == sequence[0]) | (taker == sequence[0]) | (sizes[taker] == 0), 0, jnp.maximum(slack, 0))
    shifted = jax.random.randint(jax.random.fold_in(own, 4), (count // 2,), 0, 1 << 20) % (slack + 1)
    sizes = sizes.at[giver].add(-shifted).at[taker].add(shifted)
    items = jnp.searchsorted(jnp.cumsum(sizes), jnp.arange(rows * top), side="right").astype(jnp.int32)
    listing = items.reshape(top, rows).T
    listing = listing[jax.random.permutation(jax.random.fold_in(own, 1), rows)]
    turn = jax.random.randint(jax.random.fold_in(own, 2), (rows, 1), 0, top)
    return jnp.take_along_axis(listing, (jnp.arange(top)[None, :] + turn) % top, axis=1)


def shares(count, total, bound, slope, full):
    portions = [(1 << 20) // math.isqrt(standing ** slope) + 1 for standing in range(1, count + 1)]
    largest = bound if full else min(bound, max(-(-total // count), total * portions[0] // sum(portions)))
    least = 1 if total - largest >= count - 1 else 0
    counts, spare = [largest] + [least] * (count - 1), total - largest - least * (count - 1)
    while spare > 0:
        movable = [i for i in range(1, count) if counts[i] < largest] or [i for i in range(1, count) if counts[i] < bound]
        mass, left = sum([portions[i] for i in movable]), spare
        for i in movable:
            addition = min(bound - counts[i], max(1, left * portions[i] // mass), spare)
            counts[i] = counts[i] + addition
            spare = spare - addition
    return np.array(counts)


def bell_draw(own_key, dims, width, reach, pieces=(), kind=jnp.bfloat16):
    values = width * jax.random.normal(own_key, dims, jnp.float32)
    if pieces:
        values = values * block_levels(own_key, dims, pieces, -0.22, 0.18)
    return jnp.clip(values, -reach, reach).astype(kind)


def setup_inputs(seed: int = 0, part: int = 0) -> dict:
    seeds = jax.random.split(jax.random.key(seed), 13)
    part_keys = jax.random.split(jax.random.fold_in(seeds[12], part), 13)
    hidden = bell_draw(part_keys[0], (ROWS, D), 1.0, 6.0, ((0, 16),))
    queries = draw_queries(jax.random.fold_in(jax.random.fold_in(seeds[12], part), 71), part)
    latent_cache = draw_latent_cache(jax.random.fold_in(jax.random.fold_in(seeds[12], part), 71), part)
    cache_lengths = draw_cache_lengths(jax.random.fold_in(jax.random.fold_in(seeds[12], part), 71), part)
    value_up = bell_draw(seeds[4], (HEADS, LAT, VDIM), LAT ** -0.5, 0.25, ((0, 16),))
    out_proj = bell_draw(seeds[5], (HEADS * VDIM, D), (HEADS * VDIM) ** -0.5, 0.046875, ((0, 16),))
    norm_gain = jnp.clip(1.0 + 0.18 * jax.random.normal(seeds[6], (D,), jnp.float32), 0.1, 1.9)
    expert_ids_keys = jax.random.split(jax.random.fold_in(part_keys[7], 1), ROWS // ROWS_DEV)
    expert_ids_turns = jax.random.permutation(jax.random.fold_in(part_keys[7], 3), ROWS // ROWS_DEV)
    expert_ids = jax.vmap(lambda own, number: deal_out(jax.random.fold_in(part_keys[7], 2), own, number, ROWS_DEV, EXPERTS, TOPK, ROWS_DEV, 2))(expert_ids_keys, expert_ids_turns).reshape((ROWS, TOPK))
    gate_weights = jnp.clip(0.05 + 0.45 * jax.random.uniform(part_keys[8], (ROWS, TOPK), jnp.float32) ** block_levels(part_keys[8], (ROWS, TOPK), ((0, 16),), -0.2, 0.2), 0.05, 0.5)
    gate_proj = bell_draw(seeds[9], (SPLIT * EXPERTS, DSL, FF), D ** -0.5, 0.0625, ((0, 16),))
    up_proj = bell_draw(seeds[10], (SPLIT * EXPERTS, DSL, FF), D ** -0.5, 0.0625, ((0, 16),))
    down_proj = bell_draw(seeds[11], (SPLIT * EXPERTS, FF, DSL), FF ** -0.5, 0.1875, ((0, 16),))
    return dict(hidden=hidden, queries=queries, latent_cache=latent_cache, cache_lengths=cache_lengths, value_up=value_up, out_proj=out_proj, norm_gain=norm_gain, expert_ids=expert_ids, gate_weights=gate_weights, gate_proj=gate_proj, up_proj=up_proj, down_proj=down_proj)


score_scale = 0.07216878364870323
norm_eps = 1e-06

def attend(row_args):
    row_query, row_cache, row_length = row_args
    scores = jnp.dot(row_query, row_cache.T, preferred_element_type=jnp.float32) * score_scale
    live_mask = jnp.arange(CTX, dtype=jnp.int32) < row_length
    scores = jnp.where(live_mask[None, :], scores, -jnp.inf)
    row_peak = lax.optimization_barrier(jnp.max(scores, axis=1, keepdims=True))
    exp_scores = jnp.exp(scores - row_peak)
    soft_weights = (exp_scores / lax.optimization_barrier(jnp.sum(exp_scores, axis=1, keepdims=True))).astype(jnp.bfloat16)
    return jnp.dot(soft_weights, row_cache[:, :LAT], preferred_element_type=jnp.float32).astype(jnp.bfloat16)

def reference(hidden, queries, latent_cache, cache_lengths, value_up, out_proj, norm_gain, expert_ids, gate_weights, gate_proj, up_proj, down_proj):
    latent_out = lax.map(attend, (queries, latent_cache, cache_lengths))
    head_out = jnp.einsum('rhl,hlv->rhv', latent_out.astype(jnp.float32), value_up.astype(jnp.float32)).astype(jnp.bfloat16)
    attention = jnp.dot(head_out.reshape(ROWS, HEADS * VDIM), out_proj, preferred_element_type=jnp.float32)
    residual = hidden.astype(jnp.float32) + attention
    inv_rms = lax.rsqrt(lax.optimization_barrier(jnp.mean(residual * residual, axis=1, keepdims=True)) + norm_eps)
    moe_in = (residual * inv_rms * norm_gain[None, :]).astype(jnp.bfloat16)
    gate_full = gate_proj.reshape(SPLIT, EXPERTS, DSL, FF).transpose(1, 0, 2, 3).reshape(EXPERTS, D, FF)
    up_full = up_proj.reshape(SPLIT, EXPERTS, DSL, FF).transpose(1, 0, 2, 3).reshape(EXPERTS, D, FF)
    down_full = down_proj.reshape(SPLIT, EXPERTS, FF, DSL).transpose(1, 2, 0, 3).reshape(EXPERTS, FF, D)

    def expert_mlp(mats):
        gate_mat, up_mat, down_mat = mats
        gate_act = jnp.dot(moe_in, gate_mat, preferred_element_type=jnp.float32)
        up_act = jnp.dot(moe_in, up_mat, preferred_element_type=jnp.float32)
        units = (jax.nn.silu(gate_act) * up_act).astype(jnp.bfloat16)
        return jnp.dot(units, down_mat, preferred_element_type=jnp.float32).astype(jnp.bfloat16)
    stacked = lax.map(expert_mlp, (gate_full, up_full, down_full))
    one_hot = (expert_ids[:, :, None] == jnp.arange(EXPERTS, dtype=jnp.int32)[None, None, :]).astype(jnp.float32)
    weights_full = lax.optimization_barrier(jnp.sum(gate_weights[:, :, None] * one_hot, axis=1))
    routed_sum = jnp.einsum('re,erd->rd', weights_full, stacked.astype(jnp.float32))
    return (residual + routed_sum).astype(jnp.bfloat16)
```

```python
import functools

import jax
import jax.numpy as jnp
from jax import lax
from jax.experimental import pallas as pl
from jax.experimental.pallas import tpu as pltpu
from jax.sharding import PartitionSpec as P

EXPERTS = 16


score_scale = 0.07216878364870323
norm_eps = 1e-06


def partner(value, axis, bit):
    return lax.ppermute(value, axis, [(i, i ^ 1 << bit) for i in range(lax.axis_size(axis))])


def attend_and_project(hidden, queries, latent_cache, cache_lengths, value_up, out_proj):
    latent = value_up.shape[1]
    scores = (
        jnp.einsum("rhk,rtk->rht", queries, latent_cache, preferred_element_type=jnp.float32)
        * score_scale
    )
    positions = lax.broadcasted_iota(jnp.int32, scores.shape, 2)
    scores = jnp.where(positions < cache_lengths[:, None, None], scores, -jnp.inf)
    row_peak = jnp.max(scores, axis=2, keepdims=True)
    exp_scores = jnp.exp(scores - row_peak)
    soft_weights = (exp_scores / jnp.sum(exp_scores, axis=2, keepdims=True)).astype(jnp.bfloat16)
    latent_out = jnp.einsum(
        "rht,rtl->rhl",
        soft_weights,
        latent_cache[:, :, :latent],
        preferred_element_type=jnp.float32,
    ).astype(jnp.bfloat16)
    by_head = lax.all_to_all(latent_out, "ep", split_axis=1, concat_axis=0, tiled=True)
    head_out = jnp.einsum(
        "rhl,hlv->rhv", by_head, value_up, preferred_element_type=jnp.float32
    ).astype(jnp.bfloat16)
    head_rows = head_out.reshape(head_out.shape[0], head_out.shape[1] * head_out.shape[2])
    attention = lax.psum_scatter(
        jnp.dot(head_rows, out_proj, preferred_element_type=jnp.float32),
        "ep",
        scatter_dimension=0,
        tiled=True,
    )
    return hidden.astype(jnp.float32) + attention


def on_device(
    hidden,
    queries,
    latent_cache,
    cache_lengths,
    value_up,
    out_proj,
    norm_gain,
    expert_ids,
    gate_weights,
    gate_proj,
    up_proj,
    down_proj,
):
    rows_dev = hidden.shape[0]
    ep_size = lax.axis_size("ep")
    residual = attend_and_project(hidden, queries, latent_cache, cache_lengths, value_up, out_proj)
    inv_rms = lax.rsqrt(jnp.mean(residual * residual, axis=1, keepdims=True) + norm_eps)
    moe_in = (residual * inv_rms * norm_gain[None, :]).astype(jnp.bfloat16)
    split_ways = ep_size // EXPERTS
    slice_width = moe_in.shape[1] // split_ways
    experts_iota = lax.broadcasted_iota(jnp.int32, (1, 1, EXPERTS), 2)
    member = jnp.sum((expert_ids[:, :, None] == experts_iota).astype(jnp.int32), axis=1)
    before = jnp.cumsum(member, axis=0) - member
    slot_of = jnp.take_along_axis(before, expert_ids, axis=1)
    slot_iota = lax.broadcasted_iota(jnp.int32, (1, rows_dev, 1), 1)
    chosen = (member.T[:, None, :] == 1) & (before.T[:, None, :] == slot_iota)
    selection = chosen.astype(jnp.bfloat16)
    pieces = moe_in.reshape(rows_dev, split_ways, slice_width)
    outgoing = jnp.einsum(
        "ecr,rjd->jecd", selection, pieces, preferred_element_type=jnp.float32
    ).astype(jnp.bfloat16)
    outgoing = outgoing.reshape(ep_size, rows_dev, slice_width)
    incoming = lax.all_to_all(outgoing, "ep", split_axis=0, concat_axis=0, tiled=True)
    slot_rows = incoming.reshape(ep_size * rows_dev, slice_width)
    gate_act = jnp.dot(slot_rows, gate_proj[0], preferred_element_type=jnp.float32)
    up_act = jnp.dot(slot_rows, up_proj[0], preferred_element_type=jnp.float32)
    stacked = jnp.stack((gate_act, up_act))
    low_bit = EXPERTS.bit_length() - 1
    levels = split_ways.bit_length() - 1
    for swap_level in range(levels):
        stacked = stacked + partner(
            stacked.astype(jnp.bfloat16), "ep", low_bit + swap_level
        ).astype(stacked.dtype)
    hidden_units = (jax.nn.silu(stacked[0]) * stacked[1]).astype(jnp.bfloat16)
    expert_out = jnp.dot(hidden_units, down_proj[0], preferred_element_type=jnp.float32).astype(
        jnp.bfloat16
    )
    expert_out = expert_out.reshape(ep_size, rows_dev, slice_width)
    returned = lax.all_to_all(expert_out, "ep", split_axis=0, concat_axis=0, tiled=True)
    full_rows = returned.reshape(split_ways, EXPERTS, rows_dev, slice_width).transpose(1, 2, 0, 3)
    full_rows = full_rows.reshape(EXPERTS * rows_dev, split_ways * slice_width)
    picked = jnp.take(full_rows, expert_ids * rows_dev + slot_of, axis=0)
    routed_sum = jnp.sum(gate_weights[:, :, None] * picked.astype(jnp.float32), axis=1)
    return (residual + routed_sum).astype(jnp.bfloat16)


PLANE = 4
CHUNKS = 4
TILE = 256


def remote(src, dst, send_sem, recv_sem, peer):
    return pltpu.make_async_remote_copy(
        src_ref=src,
        dst_ref=dst,
        send_sem=send_sem,
        recv_sem=recv_sem,
        device_id={"ep": peer},
        device_id_type=pl.DeviceIdType.MESH,
    )


def fused_kernel(
    n,
    hidden,
    queries,
    cache,
    lengths,
    value_up,
    out_proj,
    gain,
    ids,
    weights,
    gate_proj,
    up_proj,
    down_proj,
    out,
    q_buf,
    c_buf,
    vu_buf,
    w_buf,
    g_buf,
    u_buf,
    lat_send,
    lat_recv,
    lat_f32,
    heads,
    part_f32,
    a_send,
    a_recv,
    b_f32,
    b_send,
    b_recv,
    residual,
    own_rows,
    z_recv,
    p_f32,
    p_send,
    p_recv,
    info_own,
    info_all,
    info_rows,
    g_acc,
    u_acc,
    units,
    load_sem,
    w_sem,
    gu_sem,
    d_sem,
    lat_ss,
    lat_rs,
    a_ss,
    a_rs,
    b_ss,
    b_rs,
    z_ss,
    z_rs,
    p_ss,
    p_rs,
    i_ss,
    i_rs,
):
    me = lax.axis_index("ep")
    planes = n // PLANE
    my_q = lax.rem(me, PLANE)
    my_z = lax.div(me, PLANE)
    rows_dev, n_heads, _ = q_buf.shape
    heads_dev, latent, vdim = vu_buf.shape
    width = hidden.shape[1]
    cc = width // CHUNKS
    ctx = c_buf.shape[1]
    rows = n * rows_dev
    prows = planes * rows_dev
    bf16, f32 = jnp.bfloat16, jnp.float32

    def plane_peer(k):
        return my_z * PLANE + lax.rem(my_q + k, PLANE)

    def z_peer(k):
        return lax.rem(my_z + k, planes) * PLANE + my_q

    loads = [pltpu.make_async_copy(queries, q_buf, load_sem.at[0])]
    for r in range(rows_dev):
        loads.append(pltpu.make_async_copy(cache.at[r], c_buf.at[r], load_sem.at[1 + r]))
    load_vu = pltpu.make_async_copy(value_up, vu_buf, load_sem.at[1 + rows_dev])
    for copy in loads:
        copy.start()
    load_vu.start()

    barrier = pltpu.get_barrier_semaphore()

    @pl.loop(1, n)
    def _(k):
        pl.semaphore_signal(
            barrier,
            inc=1,
            device_id={"ep": lax.rem(me + k, n)},
            device_id_type=pl.DeviceIdType.MESH,
        )

    kd = w_buf.shape[0] // CHUNKS

    def w_copy(src, sem, i):
        span = pl.ds(i * kd, kd)
        return pltpu.make_async_copy(src.at[span, :], w_buf.at[span, :], sem.at[i])

    def gu_copy(src, dst, j, i):
        span = pl.ds(i * cc, cc)
        return pltpu.make_async_copy(src.at[0, span, :], dst.at[span, :], gu_sem.at[j, i])

    loads[0].wait()
    for r in range(rows_dev):
        loads[1 + r].wait()
        if r == rows_dev - 1:
            for i in range(CHUNKS):
                w_copy(out_proj, w_sem, i).start()
            for i in range(CHUNKS):
                gu_copy(gate_proj, g_buf, 0, i).start()
                gu_copy(up_proj, u_buf, 1, i).start()
        scores = (
            lax.dot_general(
                q_buf[r], c_buf[r], (((1,), (1,)), ((), ())), preferred_element_type=f32
            )
            * score_scale
        )
        positions = lax.broadcasted_iota(jnp.int32, scores.shape, 1)
        scores = jnp.where(positions < lengths[r], scores, -jnp.inf)
        peak = jnp.max(scores, axis=1, keepdims=True)
        expd = jnp.exp(scores - peak)
        total = jnp.sum(expd, axis=1, keepdims=True)
        acc = jnp.dot(expd.astype(bf16), c_buf[r, :, :latent], preferred_element_type=f32)
        acc = acc / total
        for d in range(n):
            lat_send[r, d] = acc[d * heads_dev : (d + 1) * heads_dev].astype(bf16)
        if r == 0:
            pl.semaphore_wait(barrier, n - 1)
        slot = my_q * prows + my_z * rows_dev + r

        @pl.loop(1, n)
        def _(k):
            peer = lax.rem(me + k, n)
            remote(
                lat_send.at[r, peer], lat_recv.at[slot], lat_ss.at[r, k], lat_rs.at[r, k], peer
            ).start()

        lat_recv[slot] = lat_send[r, me]

    lane = lax.broadcasted_iota(jnp.int32, (rows_dev, 128), 1)
    info = jnp.zeros((rows_dev, 128), f32)
    for k in range(ids.shape[1]):
        info = info + jnp.where(lane == ids[:, k : k + 1], weights[:, k : k + 1], 0.0)

    load_vu.wait()
    for r in range(rows_dev):

        @pl.loop(1, n)
        def _(k):
            peer = lax.rem(me + n - k, n)
            slot = lax.rem(peer, PLANE) * prows + lax.div(peer, PLANE) * rows_dev + r
            remote(
                lat_send.at[r, peer], lat_recv.at[slot], lat_ss.at[r, k], lat_rs.at[r, k], peer
            ).wait_recv()

    for i in range(rows):
        block = lat_recv[i].astype(f32)
        for j in range(latent // 128):
            lat_f32[j, i * heads_dev : (i + 1) * heads_dev, :] = block[:, j * 128 : (j + 1) * 128]
    for h in range(heads_dev):
        lhs = jnp.concatenate(
            [lat_f32[j, pl.ds(h, rows, stride=heads_dev), :] for j in range(latent // 128)], axis=1
        ).astype(bf16)
        heads[:, h * vdim : (h + 1) * vdim] = jnp.dot(
            lhs, vu_buf[h], preferred_element_type=f32
        ).astype(bf16)

    def stage_a(which, c, lhs, row_scale):
        @pl.loop(0, cc // TILE)
        def _(t):
            inner = pl.ds(pl.multiple_of(t * TILE, TILE), TILE)
            cols = pl.ds(pl.multiple_of(c * cc + t * TILE, TILE), TILE)
            part = jnp.dot(lhs[...], w_buf[:, cols], preferred_element_type=f32)
            if row_scale is not None:
                part = part * row_scale
            for q in range(PLANE):
                piece = part[q * prows : (q + 1) * prows]
                part_f32[c, q, :, inner] = piece
                a_send[which, c, q, :, inner] = piece.astype(bf16)

        for k in range(1, PLANE):
            a_copy(which, c, k).start()

    def a_copy(which, c, k):
        return remote(
            a_send.at[which, c, lax.rem(my_q + k, PLANE)],
            a_recv.at[which, c, k - 1],
            a_ss.at[which, c, k - 1],
            a_rs.at[which, c, k - 1],
            plane_peer(k),
        )

    def stage_b(which, c):
        total = part_f32[c, my_q]
        for k in range(1, PLANE):
            a_copy(which, c, k).wait_recv()
            total = total + a_recv[which, c, k - 1].astype(f32)
        for z in range(planes):
            piece = total[z * rows_dev : (z + 1) * rows_dev]
            b_f32[c, z] = piece
            b_send[which, c, z] = piece.astype(bf16)
        for k in range(1, planes):
            b_copy(which, c, k).start()

    def b_copy(which, c, k):
        return remote(
            b_send.at[which, c, lax.rem(my_z + k, planes)],
            b_recv.at[which, c, k - 1],
            b_ss.at[which, c, k - 1],
            b_rs.at[which, c, k - 1],
            z_peer(k),
        )

    def stage_sum(which, c):
        total = b_f32[c, my_z]
        for k in range(1, planes):
            b_copy(which, c, k).wait_recv()
            total = total + b_recv[which, c, k - 1].astype(f32)
        return total

    def z_copy(c, k):
        return remote(
            own_rows.at[c], z_recv.at[c, my_z], z_ss.at[c, k - 1], z_rs.at[c, k - 1], z_peer(k)
        )

    def z_arrival(c, k):
        return remote(
            own_rows.at[c],
            z_recv.at[c, lax.rem(my_z + planes - k, planes)],
            z_ss.at[c, k - 1],
            z_rs.at[c, k - 1],
            z_peer(k),
        )

    def p_copy(c, k):
        return remote(
            p_send.at[c], p_recv.at[c, my_q], p_ss.at[c, k - 1], p_rs.at[c, k - 1], plane_peer(k)
        )

    def p_arrival(c, k):
        return remote(
            p_send.at[c],
            p_recv.at[c, lax.rem(my_q + PLANE - k, PLANE)],
            p_ss.at[c, k - 1],
            p_rs.at[c, k - 1],
            plane_peer(k),
        )

    for i in range(CHUNKS):
        w_copy(out_proj, w_sem, i).wait()
    for c in range(CHUNKS):
        stage_a(0, c, heads, None)
    for i in range(CHUNKS):
        w_copy(down_proj.at[0], d_sem, i).start()
    for c in range(CHUNKS):
        stage_b(0, c)
    square = jnp.zeros((rows_dev, 1), f32)
    for c in range(CHUNKS):
        cols = slice(c * cc, (c + 1) * cc)
        value = hidden[:, cols].astype(f32) + stage_sum(0, c)
        residual[c] = value
        square = square + jnp.sum(value * value, axis=1, keepdims=True)
        scaled = (value * gain[:, cols]).astype(bf16)
        own_rows[c] = scaled
        for k in range(1, planes):
            z_copy(c, k).start()
        z_recv[c, my_z] = scaled
    inv_rms = lax.rsqrt(square * (1.0 / width) + norm_eps)
    info_own[...] = jnp.where(lane == 127, inv_rms, info)
    my_slot = my_q * planes + my_z

    @pl.loop(1, n)
    def _(k):
        remote(
            info_own, info_all.at[my_slot], i_ss.at[k], i_rs.at[k], lax.rem(me + k, n)
        ).start()

    info_all[my_slot] = info_own[...]
    for c in range(CHUNKS):
        for k in range(1, planes):
            z_arrival(c, k).wait_recv()
        for z in range(planes):
            p_f32[c, z * rows_dev : (z + 1) * rows_dev, :] = z_recv[c, z].astype(f32)
        block = p_f32[c].astype(bf16)
        p_send[c] = block
        for k in range(1, PLANE):
            p_copy(c, k).start()
        p_recv[c, my_q] = block

    for c in range(CHUNKS):
        gu_copy(gate_proj, g_buf, 0, c).wait()
        gu_copy(up_proj, u_buf, 1, c).wait()
        for k in range(1, PLANE):
            p_arrival(c, k).wait_recv()
        x = jnp.concatenate([p_recv[c, q].astype(f32) for q in range(PLANE)], axis=0).astype(bf16)

        @pl.loop(0, g_acc.shape[1] // TILE)
        def _(t):
            cols = pl.ds(pl.multiple_of(t * TILE, TILE), TILE)
            span = slice(c * cc, (c + 1) * cc)
            g = jnp.dot(x, g_buf[span, cols], preferred_element_type=f32)
            u = jnp.dot(x, u_buf[span, cols], preferred_element_type=f32)
            if c > 0:
                g = g + g_acc[:, cols]
                u = u + u_acc[:, cols]
            g_acc[:, cols] = g
            u_acc[:, cols] = u

    @pl.loop(1, n)
    def _(k):
        peer = lax.rem(me + n - k, n)
        slot = lax.rem(peer, PLANE) * planes + lax.div(peer, PLANE)
        remote(info_own, info_all.at[slot], i_ss.at[k], i_rs.at[k], peer).wait_recv()

    for i in range(n):
        info_rows[i * rows_dev : (i + 1) * rows_dev, :] = info_all[i]
    info = info_rows[...]
    lane = lax.broadcasted_iota(jnp.int32, info.shape, 1)
    row_inv = info[:, 127:128]
    row_weight = jnp.sum(jnp.where(lane == me, info, 0.0), axis=1, keepdims=True)
    gate = g_acc[...] * row_inv
    units[...] = (gate / (1.0 + jnp.exp(-gate)) * (u_acc[...] * row_inv)).astype(bf16)
    for i in range(CHUNKS):
        w_copy(down_proj.at[0], d_sem, i).wait()
    for c in range(CHUNKS):
        stage_a(1, c, units, row_weight)
    for c in range(CHUNKS):
        stage_b(1, c)
    for c in range(CHUNKS):
        out[:, c * cc : (c + 1) * cc] = (residual[c] + stage_sum(1, c)).astype(bf16)

    for r in range(rows_dev):

        @pl.loop(1, n)
        def _(k):
            peer = lax.rem(me + k, n)
            remote(
                lat_send.at[r, peer], lat_recv.at[0], lat_ss.at[r, k], lat_rs.at[r, k], peer
            ).wait_send()

    @pl.loop(1, n)
    def _(k):
        remote(
            info_own, info_all.at[0], i_ss.at[k], i_rs.at[k], lax.rem(me + k, n)
        ).wait_send()

    for c in range(CHUNKS):
        for which in range(2):
            for k in range(1, PLANE):
                a_copy(which, c, k).wait_send()
            for k in range(1, planes):
                b_copy(which, c, k).wait_send()
        for k in range(1, planes):
            z_copy(c, k).wait_send()
        for k in range(1, PLANE):
            p_copy(c, k).wait_send()


def fused_on_device(
    hidden,
    queries,
    latent_cache,
    cache_lengths,
    value_up,
    out_proj,
    norm_gain,
    expert_ids,
    gate_weights,
    gate_proj,
    up_proj,
    down_proj,
):
    n = lax.axis_size("ep")
    planes = n // PLANE
    rows_dev, width = hidden.shape
    rows, prows = n * rows_dev, planes * rows_dev
    heads_dev, latent, vdim = value_up.shape
    ff = gate_proj.shape[2]
    cc = width // CHUNKS
    bf16, f32 = jnp.bfloat16, jnp.float32
    vmem, anyspace = pl.BlockSpec(memory_space=pltpu.VMEM), pl.BlockSpec(memory_space=pl.ANY)
    dma = pltpu.SemaphoreType.DMA
    return pl.pallas_call(
        functools.partial(fused_kernel, n),
        out_shape=jax.ShapeDtypeStruct(hidden.shape, bf16),
        in_specs=[
            vmem,
            anyspace,
            anyspace,
            pl.BlockSpec(memory_space=pltpu.SMEM),
            anyspace,
            anyspace,
            vmem,
            vmem,
            vmem,
            anyspace,
            anyspace,
            anyspace,
        ],
        out_specs=vmem,
        scratch_shapes=[
            pltpu.VMEM(queries.shape, bf16),
            pltpu.VMEM(latent_cache.shape, bf16),
            pltpu.VMEM(value_up.shape, bf16),
            pltpu.VMEM(out_proj.shape, bf16),
            pltpu.VMEM(gate_proj.shape[1:], bf16),
            pltpu.VMEM(up_proj.shape[1:], bf16),
            pltpu.VMEM((rows_dev, n, heads_dev, latent), bf16),
            pltpu.VMEM((rows, heads_dev, latent), bf16),
            pltpu.VMEM((latent // 128, rows * heads_dev, 128), f32),
            pltpu.VMEM((rows, heads_dev * vdim), bf16),
            pltpu.VMEM((CHUNKS, PLANE, prows, cc), f32),
            pltpu.VMEM((2, CHUNKS, PLANE, prows, cc), bf16),
            pltpu.VMEM((2, CHUNKS, PLANE - 1, prows, cc), bf16),
            pltpu.VMEM((CHUNKS, planes, rows_dev, cc), f32),
            pltpu.VMEM((2, CHUNKS, planes, rows_dev, cc), bf16),
            pltpu.VMEM((2, CHUNKS, planes - 1, rows_dev, cc), bf16),
            pltpu.VMEM((CHUNKS, rows_dev, cc), f32),
            pltpu.VMEM((CHUNKS, rows_dev, cc), bf16),
            pltpu.VMEM((CHUNKS, planes, rows_dev, cc), bf16),
            pltpu.VMEM((CHUNKS, prows, cc), f32),
            pltpu.VMEM((CHUNKS, prows, cc), bf16),
            pltpu.VMEM((CHUNKS, PLANE, prows, cc), bf16),
            pltpu.VMEM((rows_dev, 128), f32),
            pltpu.VMEM((n, rows_dev, 128), f32),
            pltpu.VMEM((rows, 128), f32),
            pltpu.VMEM((rows, ff), f32),
            pltpu.VMEM((rows, ff), f32),
            pltpu.VMEM((rows, ff), bf16),
            dma((2 + rows_dev,)),
            dma((CHUNKS,)),
            dma((2, CHUNKS)),
            dma((CHUNKS,)),
            dma((rows_dev, n)),
            dma((rows_dev, n)),
            dma((2, CHUNKS, PLANE - 1)),
            dma((2, CHUNKS, PLANE - 1)),
            dma((2, CHUNKS, planes - 1)),
            dma((2, CHUNKS, planes - 1)),
            dma((CHUNKS, planes - 1)),
            dma((CHUNKS, planes - 1)),
            dma((CHUNKS, PLANE - 1)),
            dma((CHUNKS, PLANE - 1)),
            dma((n,)),
            dma((n,)),
        ],
        compiler_params=pltpu.CompilerParams(
            collective_id=0, has_side_effects=True, vmem_limit_bytes=67043328
        ),
        name="fused_layer",
    )(
        hidden,
        queries,
        latent_cache,
        cache_lengths,
        value_up,
        out_proj,
        norm_gain[None, :],
        expert_ids,
        gate_weights,
        gate_proj,
        up_proj,
        down_proj,
    )


def solution(mesh):
    body = fused_on_device if mesh.shape["ep"] == EXPERTS else on_device
    return jax.shard_map(
        body,
        mesh=mesh,
        in_specs=(
            P(("groups", "ep"), None),
            P(("groups", "ep"), None, None),
            P(("groups", "ep"), None, None),
            P(("groups", "ep")),
            P("ep", None, None),
            P("ep", None),
            P(),
            P(("groups", "ep"), None),
            P(("groups", "ep"), None),
            P("ep", None, None),
            P("ep", None, None),
            P("ep", None, None),
        ),
        out_specs=P(("groups", "ep"), None),
        check_vma=False,
    )
```

```python
import functools

import jax
import jax.numpy as jnp
from jax import lax
from jax.experimental import pallas as pl
from jax.experimental.pallas import tpu as pltpu
from jax.sharding import PartitionSpec as P

EXPERTS = 16


score_scale = 0.07216878364870323
norm_eps = 1e-06


def partner(value, axis, bit):
    return lax.ppermute(value, axis, [(i, i ^ 1 << bit) for i in range(lax.axis_size(axis))])


def attend_and_project(hidden, queries, latent_cache, cache_lengths, value_up, out_proj):
    latent = value_up.shape[1]
    scores = (
        jnp.einsum("rhk,rtk->rht", queries, latent_cache, preferred_element_type=jnp.float32)
        * score_scale
    )
    positions = lax.broadcasted_iota(jnp.int32, scores.shape, 2)
    scores = jnp.where(positions < cache_lengths[:, None, None], scores, -jnp.inf)
    row_peak = jnp.max(scores, axis=2, keepdims=True)
    exp_scores = jnp.exp(scores - row_peak)
    soft_weights = (exp_scores / jnp.sum(exp_scores, axis=2, keepdims=True)).astype(jnp.bfloat16)
    latent_out = jnp.einsum(
        "rht,rtl->rhl",
        soft_weights,
        latent_cache[:, :, :latent],
        preferred_element_type=jnp.float32,
    ).astype(jnp.bfloat16)
    by_head = lax.all_to_all(latent_out, "ep", split_axis=1, concat_axis=0, tiled=True)
    head_out = jnp.einsum(
        "rhl,hlv->rhv", by_head, value_up, preferred_element_type=jnp.float32
    ).astype(jnp.bfloat16)
    head_rows = head_out.reshape(head_out.shape[0], head_out.shape[1] * head_out.shape[2])
    attention = lax.psum_scatter(
        jnp.dot(head_rows, out_proj, preferred_element_type=jnp.float32),
        "ep",
        scatter_dimension=0,
        tiled=True,
    )
    return hidden.astype(jnp.float32) + attention


def on_device(
    hidden,
    queries,
    latent_cache,
    cache_lengths,
    value_up,
    out_proj,
    norm_gain,
    expert_ids,
    gate_weights,
    gate_proj,
    up_proj,
    down_proj,
):
    rows_dev = hidden.shape[0]
    ep_size = lax.axis_size("ep")
    residual = attend_and_project(hidden, queries, latent_cache, cache_lengths, value_up, out_proj)
    inv_rms = lax.rsqrt(jnp.mean(residual * residual, axis=1, keepdims=True) + norm_eps)
    moe_in = (residual * inv_rms * norm_gain[None, :]).astype(jnp.bfloat16)
    split_ways = ep_size // EXPERTS
    slice_width = moe_in.shape[1] // split_ways
    experts_iota = lax.broadcasted_iota(jnp.int32, (1, 1, EXPERTS), 2)
    member = jnp.sum((expert_ids[:, :, None] == experts_iota).astype(jnp.int32), axis=1)
    before = jnp.cumsum(member, axis=0) - member
    slot_of = jnp.take_along_axis(before, expert_ids, axis=1)
    slot_iota = lax.broadcasted_iota(jnp.int32, (1, rows_dev, 1), 1)
    chosen = (member.T[:, None, :] == 1) & (before.T[:, None, :] == slot_iota)
    selection = chosen.astype(jnp.bfloat16)
    pieces = moe_in.reshape(rows_dev, split_ways, slice_width)
    outgoing = jnp.einsum(
        "ecr,rjd->jecd", selection, pieces, preferred_element_type=jnp.float32
    ).astype(jnp.bfloat16)
    outgoing = outgoing.reshape(ep_size, rows_dev, slice_width)
    incoming = lax.all_to_all(outgoing, "ep", split_axis=0, concat_axis=0, tiled=True)
    slot_rows = incoming.reshape(ep_size * rows_dev, slice_width)
    gate_act = jnp.dot(slot_rows, gate_proj[0], preferred_element_type=jnp.float32)
    up_act = jnp.dot(slot_rows, up_proj[0], preferred_element_type=jnp.float32)
    stacked = jnp.stack((gate_act, up_act))
    low_bit = EXPERTS.bit_length() - 1
    levels = split_ways.bit_length() - 1
    for swap_level in range(levels):
        stacked = stacked + partner(
            stacked.astype(jnp.bfloat16), "ep", low_bit + swap_level
        ).astype(stacked.dtype)
    hidden_units = (jax.nn.silu(stacked[0]) * stacked[1]).astype(jnp.bfloat16)
    expert_out = jnp.dot(hidden_units, down_proj[0], preferred_element_type=jnp.float32).astype(
        jnp.bfloat16
    )
    expert_out = expert_out.reshape(ep_size, rows_dev, slice_width)
    returned = lax.all_to_all(expert_out, "ep", split_axis=0, concat_axis=0, tiled=True)
    full_rows = returned.reshape(split_ways, EXPERTS, rows_dev, slice_width).transpose(1, 2, 0, 3)
    full_rows = full_rows.reshape(EXPERTS * rows_dev, split_ways * slice_width)
    picked = jnp.take(full_rows, expert_ids * rows_dev + slot_of, axis=0)
    routed_sum = jnp.sum(gate_weights[:, :, None] * picked.astype(jnp.float32), axis=1)
    return (residual + routed_sum).astype(jnp.bfloat16)


PLANE = 4
LOADS = 4


def chunks_of(width):
    return next(m for m in (7, 8, 4, 2, 1) if width % (m * 128) == 0)


def step_order(chunks, spans):
    ready = [(c * spans[0], 0, c) for c in range(chunks)]
    for stage in range(1, len(spans)):
        delay = sum(spans[1 : stage + 1])
        ready += [((c + 1) * spans[0] + delay, stage, c) for c in range(chunks)]
    return [(stage, c) for _, stage, c in sorted(ready)]


def remote(src, dst, send_sem, recv_sem, peer):
    return pltpu.make_async_remote_copy(
        src_ref=src,
        dst_ref=dst,
        send_sem=send_sem,
        recv_sem=recv_sem,
        device_id={"ep": peer},
        device_id_type=pl.DeviceIdType.MESH,
    )


def fused_kernel(
    n,
    hidden,
    queries,
    cache,
    lengths,
    value_up,
    out_proj,
    gain,
    ids,
    weights,
    gate_proj,
    up_proj,
    down_proj,
    out,
    q_buf,
    c_buf,
    vu_buf,
    w_buf,
    g_buf,
    u_buf,
    lat_send,
    lat_recv,
    lat_f32,
    heads,
    part_f32,
    a_send,
    a_recv,
    b_f32,
    b_send,
    b_recv,
    residual,
    own_rows,
    z_recv,
    p_f32,
    p_send,
    p_recv,
    info_own,
    info_all,
    info_rows,
    g_acc,
    u_acc,
    units,
    load_sem,
    w_sem,
    gu_sem,
    d_sem,
    lat_ss,
    lat_rs,
    a_ss,
    a_rs,
    b_ss,
    b_rs,
    z_ss,
    z_rs,
    p_ss,
    p_rs,
    i_ss,
    i_rs,
):
    me = lax.axis_index("ep")
    planes = n // PLANE
    my_q = lax.rem(me, PLANE)
    my_z = lax.div(me, PLANE)
    rows_dev = q_buf.shape[0]
    heads_dev, latent, vdim = vu_buf.shape
    width = hidden.shape[1]
    chunks = chunks_of(width)
    cc = width // chunks
    rows = n * rows_dev
    prows = planes * rows_dev
    bf16, f32 = jnp.bfloat16, jnp.float32

    def plane_peer(k):
        return my_z * PLANE + lax.rem(my_q + k, PLANE)

    def z_peer(k):
        return lax.rem(my_z + k, planes) * PLANE + my_q

    loads = [pltpu.make_async_copy(queries, q_buf, load_sem.at[0])]
    for r in range(rows_dev):
        loads.append(pltpu.make_async_copy(cache.at[r], c_buf.at[r], load_sem.at[1 + r]))
    load_vu = pltpu.make_async_copy(value_up, vu_buf, load_sem.at[1 + rows_dev])
    for copy in loads:
        copy.start()
    load_vu.start()

    barrier = pltpu.get_barrier_semaphore()

    @pl.loop(1, n)
    def _(k):
        pl.semaphore_signal(
            barrier,
            inc=1,
            device_id={"ep": lax.rem(me + k, n)},
            device_id_type=pl.DeviceIdType.MESH,
        )

    kd = w_buf.shape[0] // LOADS

    def w_copy(src, sem, i):
        span = pl.ds(i * kd, kd)
        return pltpu.make_async_copy(src.at[span, :], w_buf.at[span, :], sem.at[i])

    def gu_copy(src, dst, j, i):
        span = pl.ds(i * cc, cc)
        return pltpu.make_async_copy(src.at[0, span, :], dst.at[span, :], gu_sem.at[j, i])

    loads[0].wait()
    for r in range(rows_dev):
        loads[1 + r].wait()
        if r == 0:
            for i in range(LOADS):
                w_copy(out_proj, w_sem, i).start()
        scores = (
            lax.dot_general(
                q_buf[r], c_buf[r], (((0,), (0,)), ((), ())), preferred_element_type=f32
            )
            * score_scale
        )
        positions = lax.broadcasted_iota(jnp.int32, scores.shape, 1)
        scores = jnp.where(positions < lengths[r], scores, -jnp.inf)
        peak = jnp.max(scores, axis=1, keepdims=True)
        expd = jnp.exp(scores - peak)
        total = jnp.sum(expd, axis=1, keepdims=True)
        acc = lax.dot_general(
            expd.astype(bf16),
            c_buf[r, :latent],
            (((1,), (1,)), ((), ())),
            preferred_element_type=f32,
        )
        acc = acc / total
        for d in range(n):
            lat_send[r, d] = acc[d * heads_dev : (d + 1) * heads_dev].astype(bf16)
        if r == 0:
            pl.semaphore_wait(barrier, n - 1)
        slot = my_q * prows + my_z * rows_dev + r

        @pl.loop(1, n)
        def _(k):
            peer = lax.rem(me + k, n)
            remote(
                lat_send.at[r, peer], lat_recv.at[slot], lat_ss.at[r, k], lat_rs.at[r, k], peer
            ).start()

        lat_recv[slot] = lat_send[r, me]

    lane = lax.broadcasted_iota(jnp.int32, (rows_dev, 128), 1)
    info = jnp.zeros((rows_dev, 128), f32)
    for k in range(ids.shape[1]):
        info = info + jnp.where(lane == ids[:, k : k + 1], weights[:, k : k + 1], 0.0)

    for i in range(chunks):
        gu_copy(gate_proj, g_buf, 0, i).start()
        gu_copy(up_proj, u_buf, 1, i).start()
    load_vu.wait()
    for r in range(rows_dev):

        @pl.loop(1, n)
        def _(k):
            peer = lax.rem(me + n - k, n)
            slot = lax.rem(peer, PLANE) * prows + lax.div(peer, PLANE) * rows_dev + r
            remote(
                lat_send.at[r, peer], lat_recv.at[slot], lat_ss.at[r, k], lat_rs.at[r, k], peer
            ).wait_recv()

    for i in range(rows):
        block = lat_recv[i].astype(f32)
        for j in range(latent // 128):
            lat_f32[j, i * heads_dev : (i + 1) * heads_dev, :] = block[:, j * 128 : (j + 1) * 128]
    for h in range(heads_dev):
        lhs = jnp.concatenate(
            [lat_f32[j, pl.ds(h, rows, stride=heads_dev), :] for j in range(latent // 128)], axis=1
        ).astype(bf16)
        heads[:, h * vdim : (h + 1) * vdim] = jnp.dot(
            lhs, vu_buf[h], preferred_element_type=f32
        ).astype(bf16)

    def stage_a(which, c, lhs, row_scale):
        cols = slice(c * cc, (c + 1) * cc)
        part = jnp.dot(lhs[...], w_buf[:, cols], preferred_element_type=f32)
        if row_scale is not None:
            part = part * row_scale
        for q in range(PLANE):
            piece = part[q * prows : (q + 1) * prows]
            part_f32[c, q] = piece
            a_send[which, c, q] = piece.astype(bf16)
        for k in range(1, PLANE):
            a_copy(which, c, k).start()

    def a_copy(which, c, k):
        return remote(
            a_send.at[which, c, lax.rem(my_q + k, PLANE)],
            a_recv.at[which, c, k - 1],
            a_ss.at[which, c, k - 1],
            a_rs.at[which, c, k - 1],
            plane_peer(k),
        )

    def stage_b(which, c):
        total = part_f32[c, my_q]
        for k in range(1, PLANE):
            a_copy(which, c, k).wait_recv()
            total = total + a_recv[which, c, k - 1].astype(f32)
        for z in range(planes):
            piece = total[z * rows_dev : (z + 1) * rows_dev]
            b_f32[c, z] = piece
            b_send[which, c, z] = piece.astype(bf16)
        for k in range(1, planes):
            b_copy(which, c, k).start()

    def b_copy(which, c, k):
        return remote(
            b_send.at[which, c, lax.rem(my_z + k, planes)],
            b_recv.at[which, c, k - 1],
            b_ss.at[which, c, k - 1],
            b_rs.at[which, c, k - 1],
            z_peer(k),
        )

    def stage_sum(which, c):
        total = b_f32[c, my_z]
        for k in range(1, planes):
            b_copy(which, c, k).wait_recv()
            total = total + b_recv[which, c, k - 1].astype(f32)
        return total

    def z_copy(c, k):
        return remote(
            own_rows.at[c], z_recv.at[c, my_z], z_ss.at[c, k - 1], z_rs.at[c, k - 1], z_peer(k)
        )

    def z_arrival(c, k):
        return remote(
            own_rows.at[c],
            z_recv.at[c, lax.rem(my_z + planes - k, planes)],
            z_ss.at[c, k - 1],
            z_rs.at[c, k - 1],
            z_peer(k),
        )

    def p_copy(c, k):
        return remote(
            p_send.at[c], p_recv.at[c, my_q], p_ss.at[c, k - 1], p_rs.at[c, k - 1], plane_peer(k)
        )

    def p_arrival(c, k):
        return remote(
            p_send.at[c],
            p_recv.at[c, lax.rem(my_q + PLANE - k, PLANE)],
            p_ss.at[c, k - 1],
            p_rs.at[c, k - 1],
            plane_peer(k),
        )

    my_slot = my_q * planes + my_z

    def stage_own(c, square):
        cols = slice(c * cc, (c + 1) * cc)
        value = hidden[:, cols].astype(f32) + stage_sum(0, c)
        residual[c] = value
        scaled = (value * gain[:, cols]).astype(bf16)
        own_rows[c] = scaled
        for k in range(1, planes):
            z_copy(c, k).start()
        z_recv[c, my_z] = scaled
        return square + jnp.sum(value * value, axis=1, keepdims=True)

    def send_info(square):
        inv_rms = lax.rsqrt(square * (1.0 / width) + norm_eps)
        info_own[...] = jnp.where(lane == 127, inv_rms, info)

        @pl.loop(1, n)
        def _(k):
            remote(
                info_own, info_all.at[my_slot], i_ss.at[k], i_rs.at[k], lax.rem(me + k, n)
            ).start()

        info_all[my_slot] = info_own[...]

    def stage_spread(c):
        for k in range(1, planes):
            z_arrival(c, k).wait_recv()
        for z in range(planes):
            p_f32[c, z * rows_dev : (z + 1) * rows_dev, :] = z_recv[c, z].astype(f32)
        block = p_f32[c].astype(bf16)
        p_send[c] = block
        for k in range(1, PLANE):
            p_copy(c, k).start()
        p_recv[c, my_q] = block

    def stage_units(c):
        gu_copy(gate_proj, g_buf, 0, c).wait()
        gu_copy(up_proj, u_buf, 1, c).wait()
        for k in range(1, PLANE):
            p_arrival(c, k).wait_recv()
        x = jnp.concatenate([p_recv[c, q].astype(f32) for q in range(PLANE)], axis=0).astype(bf16)
        span = slice(c * cc, (c + 1) * cc)
        for acc, mat in ((g_acc, g_buf), (u_acc, u_buf)):
            part = jnp.dot(x, mat[span, :], preferred_element_type=f32)
            acc[...] = part if c == 0 else acc[...] + part

    for i in range(LOADS):
        w_copy(out_proj, w_sem, i).wait()
    square = jnp.zeros((rows_dev, 1), f32)
    for stage, c in step_order(chunks, (0.6, 2.4, 3.5, 3.5, 2.4)):
        if stage == 0:
            stage_a(0, c, heads, None)
            if c == chunks - 1:
                for i in range(LOADS):
                    w_copy(down_proj.at[0], d_sem, i).start()
        elif stage == 1:
            stage_b(0, c)
        elif stage == 2:
            square = stage_own(c, square)
            if c == chunks - 1:
                send_info(square)
        elif stage == 3:
            stage_spread(c)
        else:
            stage_units(c)

    @pl.loop(1, n)
    def _(k):
        peer = lax.rem(me + n - k, n)
        slot = lax.rem(peer, PLANE) * planes + lax.div(peer, PLANE)
        remote(info_own, info_all.at[slot], i_ss.at[k], i_rs.at[k], peer).wait_recv()

    for i in range(n):
        info_rows[i * rows_dev : (i + 1) * rows_dev, :] = info_all[i]
    info = info_rows[...]
    lane = lax.broadcasted_iota(jnp.int32, info.shape, 1)
    row_inv = info[:, 127:128]
    row_weight = jnp.sum(jnp.where(lane == me, info, 0.0), axis=1, keepdims=True)
    gate = g_acc[...] * row_inv
    units[...] = (gate / (1.0 + jnp.exp(-gate)) * (u_acc[...] * row_inv)).astype(bf16)
    for i in range(LOADS):
        w_copy(down_proj.at[0], d_sem, i).wait()
    for stage, c in step_order(chunks, (0.6, 2.4, 3.5)):
        if stage == 0:
            stage_a(1, c, units, row_weight)
        elif stage == 1:
            stage_b(1, c)
        else:
            out[:, c * cc : (c + 1) * cc] = (residual[c] + stage_sum(1, c)).astype(bf16)

    for r in range(rows_dev):

        @pl.loop(1, n)
        def _(k):
            peer = lax.rem(me + k, n)
            remote(
                lat_send.at[r, peer], lat_recv.at[0], lat_ss.at[r, k], lat_rs.at[r, k], peer
            ).wait_send()

    @pl.loop(1, n)
    def _(k):
        remote(
            info_own, info_all.at[0], i_ss.at[k], i_rs.at[k], lax.rem(me + k, n)
        ).wait_send()

    for c in range(chunks):
        for which in range(2):
            for k in range(1, PLANE):
                a_copy(which, c, k).wait_send()
            for k in range(1, planes):
                b_copy(which, c, k).wait_send()
        for k in range(1, planes):
            z_copy(c, k).wait_send()
        for k in range(1, PLANE):
            p_copy(c, k).wait_send()


def fused_on_device(
    hidden,
    queries,
    latent_cache,
    cache_lengths,
    value_up,
    out_proj,
    norm_gain,
    expert_ids,
    gate_weights,
    gate_proj,
    up_proj,
    down_proj,
):
    n = lax.axis_size("ep")
    planes = n // PLANE
    queries = jnp.swapaxes(queries, 1, 2)
    latent_cache = jnp.swapaxes(latent_cache, 1, 2)
    rows_dev, width = hidden.shape
    rows, prows = n * rows_dev, planes * rows_dev
    heads_dev, latent, vdim = value_up.shape
    ff = gate_proj.shape[2]
    chunks = chunks_of(width)
    cc = width // chunks
    bf16, f32 = jnp.bfloat16, jnp.float32
    vmem, anyspace = pl.BlockSpec(memory_space=pltpu.VMEM), pl.BlockSpec(memory_space=pl.ANY)
    dma = pltpu.SemaphoreType.DMA
    return pl.pallas_call(
        functools.partial(fused_kernel, n),
        out_shape=jax.ShapeDtypeStruct(hidden.shape, bf16),
        in_specs=[
            vmem,
            anyspace,
            anyspace,
            pl.BlockSpec(memory_space=pltpu.SMEM),
            anyspace,
            anyspace,
            vmem,
            vmem,
            vmem,
            anyspace,
            anyspace,
            anyspace,
        ],
        out_specs=vmem,
        scratch_shapes=[
            pltpu.VMEM(queries.shape, bf16),
            pltpu.VMEM(latent_cache.shape, bf16),
            pltpu.VMEM(value_up.shape, bf16),
            pltpu.VMEM(out_proj.shape, bf16),
            pltpu.VMEM(gate_proj.shape[1:], bf16),
            pltpu.VMEM(up_proj.shape[1:], bf16),
            pltpu.VMEM((rows_dev, n, heads_dev, latent), bf16),
            pltpu.VMEM((rows, heads_dev, latent), bf16),
            pltpu.VMEM((latent // 128, rows * heads_dev, 128), f32),
            pltpu.VMEM((rows, heads_dev * vdim), bf16),
            pltpu.VMEM((chunks, PLANE, prows, cc), f32),
            pltpu.VMEM((2, chunks, PLANE, prows, cc), bf16),
            pltpu.VMEM((2, chunks, PLANE - 1, prows, cc), bf16),
            pltpu.VMEM((chunks, planes, rows_dev, cc), f32),
            pltpu.VMEM((2, chunks, planes, rows_dev, cc), bf16),
            pltpu.VMEM((2, chunks, planes - 1, rows_dev, cc), bf16),
            pltpu.VMEM((chunks, rows_dev, cc), f32),
            pltpu.VMEM((chunks, rows_dev, cc), bf16),
            pltpu.VMEM((chunks, planes, rows_dev, cc), bf16),
            pltpu.VMEM((chunks, prows, cc), f32),
            pltpu.VMEM((chunks, prows, cc), bf16),
            pltpu.VMEM((chunks, PLANE, prows, cc), bf16),
            pltpu.VMEM((rows_dev, 128), f32),
            pltpu.VMEM((n, rows_dev, 128), f32),
            pltpu.VMEM((rows, 128), f32),
            pltpu.VMEM((rows, ff), f32),
            pltpu.VMEM((rows, ff), f32),
            pltpu.VMEM((rows, ff), bf16),
            dma((2 + rows_dev,)),
            dma((LOADS,)),
            dma((2, chunks)),
            dma((LOADS,)),
            dma((rows_dev, n)),
            dma((rows_dev, n)),
            dma((2, chunks, PLANE - 1)),
            dma((2, chunks, PLANE - 1)),
            dma((2, chunks, planes - 1)),
            dma((2, chunks, planes - 1)),
            dma((chunks, planes - 1)),
            dma((chunks, planes - 1)),
            dma((chunks, PLANE - 1)),
            dma((chunks, PLANE - 1)),
            dma((n,)),
            dma((n,)),
        ],
        compiler_params=pltpu.CompilerParams(
            collective_id=0, has_side_effects=True, vmem_limit_bytes=67043328
        ),
        name="fused_layer",
    )(
        hidden,
        queries,
        latent_cache,
        cache_lengths,
        value_up,
        out_proj,
        norm_gain[None, :],
        expert_ids,
        gate_weights,
        gate_proj,
        up_proj,
        down_proj,
    )


def solution(mesh):
    body = fused_on_device if mesh.shape["ep"] == EXPERTS else on_device
    return jax.shard_map(
        body,
        mesh=mesh,
        in_specs=(
            P(("groups", "ep"), None),
            P(("groups", "ep"), None, None),
            P(("groups", "ep"), None, None),
            P(("groups", "ep")),
            P("ep", None, None),
            P("ep", None),
            P(),
            P(("groups", "ep"), None),
            P(("groups", "ep"), None),
            P("ep", None, None),
            P("ep", None, None),
            P("ep", None, None),
        ),
        out_specs=P(("groups", "ep"), None),
        check_vma=False,
    )
```

```python
import functools

import jax
import jax.numpy as jnp
from jax import lax
from jax.experimental import pallas as pl
from jax.experimental.pallas import tpu as pltpu
from jax.sharding import PartitionSpec as P

EXPERTS = 16


score_scale = 0.07216878364870323
norm_eps = 1e-06


def partner(value, axis, bit):
    return lax.ppermute(value, axis, [(i, i ^ 1 << bit) for i in range(lax.axis_size(axis))])


def attend_and_project(hidden, queries, latent_cache, cache_lengths, value_up, out_proj):
    latent = value_up.shape[1]
    scores = (
        jnp.einsum("rhk,rtk->rht", queries, latent_cache, preferred_element_type=jnp.float32)
        * score_scale
    )
    positions = lax.broadcasted_iota(jnp.int32, scores.shape, 2)
    scores = jnp.where(positions < cache_lengths[:, None, None], scores, -jnp.inf)
    row_peak = jnp.max(scores, axis=2, keepdims=True)
    exp_scores = jnp.exp(scores - row_peak)
    soft_weights = (exp_scores / jnp.sum(exp_scores, axis=2, keepdims=True)).astype(jnp.bfloat16)
    latent_out = jnp.einsum(
        "rht,rtl->rhl",
        soft_weights,
        latent_cache[:, :, :latent],
        preferred_element_type=jnp.float32,
    ).astype(jnp.bfloat16)
    by_head = lax.all_to_all(latent_out, "ep", split_axis=1, concat_axis=0, tiled=True)
    head_out = jnp.einsum(
        "rhl,hlv->rhv", by_head, value_up, preferred_element_type=jnp.float32
    ).astype(jnp.bfloat16)
    head_rows = head_out.reshape(head_out.shape[0], head_out.shape[1] * head_out.shape[2])
    attention = lax.psum_scatter(
        jnp.dot(head_rows, out_proj, preferred_element_type=jnp.float32),
        "ep",
        scatter_dimension=0,
        tiled=True,
    )
    return hidden.astype(jnp.float32) + attention


def on_device(
    hidden,
    queries,
    latent_cache,
    cache_lengths,
    value_up,
    out_proj,
    norm_gain,
    expert_ids,
    gate_weights,
    gate_proj,
    up_proj,
    down_proj,
):
    rows_dev = hidden.shape[0]
    ep_size = lax.axis_size("ep")
    residual = attend_and_project(hidden, queries, latent_cache, cache_lengths, value_up, out_proj)
    inv_rms = lax.rsqrt(jnp.mean(residual * residual, axis=1, keepdims=True) + norm_eps)
    moe_in = (residual * inv_rms * norm_gain[None, :]).astype(jnp.bfloat16)
    split_ways = ep_size // EXPERTS
    slice_width = moe_in.shape[1] // split_ways
    experts_iota = lax.broadcasted_iota(jnp.int32, (1, 1, EXPERTS), 2)
    member = jnp.sum((expert_ids[:, :, None] == experts_iota).astype(jnp.int32), axis=1)
    before = jnp.cumsum(member, axis=0) - member
    slot_of = jnp.take_along_axis(before, expert_ids, axis=1)
    slot_iota = lax.broadcasted_iota(jnp.int32, (1, rows_dev, 1), 1)
    chosen = (member.T[:, None, :] == 1) & (before.T[:, None, :] == slot_iota)
    selection = chosen.astype(jnp.bfloat16)
    pieces = moe_in.reshape(rows_dev, split_ways, slice_width)
    outgoing = jnp.einsum(
        "ecr,rjd->jecd", selection, pieces, preferred_element_type=jnp.float32
    ).astype(jnp.bfloat16)
    outgoing = outgoing.reshape(ep_size, rows_dev, slice_width)
    incoming = lax.all_to_all(outgoing, "ep", split_axis=0, concat_axis=0, tiled=True)
    slot_rows = incoming.reshape(ep_size * rows_dev, slice_width)
    gate_act = jnp.dot(slot_rows, gate_proj[0], preferred_element_type=jnp.float32)
    up_act = jnp.dot(slot_rows, up_proj[0], preferred_element_type=jnp.float32)
    stacked = jnp.stack((gate_act, up_act))
    low_bit = EXPERTS.bit_length() - 1
    levels = split_ways.bit_length() - 1
    for swap_level in range(levels):
        stacked = stacked + partner(
            stacked.astype(jnp.bfloat16), "ep", low_bit + swap_level
        ).astype(stacked.dtype)
    hidden_units = (jax.nn.silu(stacked[0]) * stacked[1]).astype(jnp.bfloat16)
    expert_out = jnp.dot(hidden_units, down_proj[0], preferred_element_type=jnp.float32).astype(
        jnp.bfloat16
    )
    expert_out = expert_out.reshape(ep_size, rows_dev, slice_width)
    returned = lax.all_to_all(expert_out, "ep", split_axis=0, concat_axis=0, tiled=True)
    full_rows = returned.reshape(split_ways, EXPERTS, rows_dev, slice_width).transpose(1, 2, 0, 3)
    full_rows = full_rows.reshape(EXPERTS * rows_dev, split_ways * slice_width)
    picked = jnp.take(full_rows, expert_ids * rows_dev + slot_of, axis=0)
    routed_sum = jnp.sum(gate_weights[:, :, None] * picked.astype(jnp.float32), axis=1)
    return (residual + routed_sum).astype(jnp.bfloat16)


PLANE = 4
LOADS = 4


def chunks_of(width):
    return next(m for m in (7, 8, 4, 2, 1) if width % (m * 128) == 0)


def step_order(chunks, spans):
    ready = [(c * spans[0], 0, c) for c in range(chunks)]
    for stage in range(1, len(spans)):
        delay = sum(spans[1 : stage + 1])
        ready += [((c + 1) * spans[0] + delay, stage, c) for c in range(chunks)]
    return [(stage, c) for _, stage, c in sorted(ready)]


def remote(src, dst, send_sem, recv_sem, peer):
    return pltpu.make_async_remote_copy(
        src_ref=src,
        dst_ref=dst,
        send_sem=send_sem,
        recv_sem=recv_sem,
        device_id={"ep": peer},
        device_id_type=pl.DeviceIdType.MESH,
    )


def fused_kernel(
    n,
    hidden_hbm,
    queries,
    cache,
    lengths_hbm,
    value_up,
    out_proj,
    gain_hbm,
    ids_hbm,
    weights_hbm,
    gate_proj,
    up_proj,
    down_proj,
    out,
    hidden,
    gain,
    ids,
    weights,
    lengths,
    q_rows,
    q_buf,
    c_buf,
    vu_buf,
    w_buf,
    g_buf,
    u_buf,
    lat_send,
    lat_recv,
    lat_f32,
    heads,
    part_f32,
    a_send,
    a_recv,
    b_f32,
    b_send,
    b_recv,
    residual,
    own_rows,
    z_recv,
    p_f32,
    p_send,
    p_recv,
    info_own,
    info_all,
    info_rows,
    g_acc,
    u_acc,
    units,
    load_sem,
    w_sem,
    gu_sem,
    d_sem,
    lat_ss,
    lat_rs,
    a_ss,
    a_rs,
    b_ss,
    b_rs,
    z_ss,
    z_rs,
    p_ss,
    p_rs,
    i_ss,
    i_rs,
):
    me = lax.axis_index("ep")
    planes = n // PLANE
    my_q = lax.rem(me, PLANE)
    my_z = lax.div(me, PLANE)
    rows_dev = q_buf.shape[0]
    heads_dev, latent, vdim = vu_buf.shape
    width = hidden.shape[1]
    chunks = chunks_of(width)
    cc = width // chunks
    rows = n * rows_dev
    prows = planes * rows_dev
    bf16, f32 = jnp.bfloat16, jnp.float32

    def plane_peer(k):
        return my_z * PLANE + lax.rem(my_q + k, PLANE)

    def z_peer(k):
        return lax.rem(my_z + k, planes) * PLANE + my_q

    loads = [pltpu.make_async_copy(queries, q_buf, load_sem.at[0])]
    for r in range(rows_dev):
        loads.append(pltpu.make_async_copy(cache.at[r], c_buf.at[r], load_sem.at[1 + r]))
    load_vu = pltpu.make_async_copy(value_up, vu_buf, load_sem.at[1 + rows_dev])
    small = [
        pltpu.make_async_copy(src, dst, load_sem.at[2 + rows_dev + i])
        for i, (src, dst) in enumerate(
            (
                (lengths_hbm, lengths),
                (ids_hbm, ids),
                (weights_hbm, weights),
                (hidden_hbm, hidden),
                (gain_hbm, gain),
            )
        )
    ]
    small[0].start()
    loads[0].start()
    loads[1].start()

    barrier = pltpu.get_barrier_semaphore()

    @pl.loop(1, n)
    def _(k):
        pl.semaphore_signal(
            barrier,
            inc=1,
            device_id={"ep": lax.rem(me + k, n)},
            device_id_type=pl.DeviceIdType.MESH,
        )

    kd = w_buf.shape[0] // LOADS

    def w_copy(src, sem, i):
        span = pl.ds(i * kd, kd)
        return pltpu.make_async_copy(src.at[span, :], w_buf.at[span, :], sem.at[i])

    def gu_copy(src, dst, j, i):
        span = pl.ds(i * cc, cc)
        return pltpu.make_async_copy(src.at[0, span, :], dst.at[span, :], gu_sem.at[j, i])

    half = n // 2
    side = lax.div(me, half)
    my_low = lax.rem(me, half)

    def attend(r, where):
        span = pl.ds(pl.multiple_of(where * half * heads_dev, half * heads_dev), half * heads_dev)
        scores = (
            jnp.dot(q_rows[r, span, :], c_buf[r], preferred_element_type=f32) * score_scale
        )
        positions = lax.broadcasted_iota(jnp.int32, scores.shape, 1)
        scores = jnp.where(positions < lengths[r], scores, -jnp.inf)
        peak = jnp.max(scores, axis=1, keepdims=True)
        expd = jnp.exp(scores - peak)
        total = jnp.sum(expd, axis=1, keepdims=True)
        acc = lax.dot_general(
            expd.astype(bf16),
            c_buf[r, :latent],
            (((1,), (1,)), ((), ())),
            preferred_element_type=f32,
        )
        acc = acc / total
        for i in range(half):
            lat_send[r, where * half + i] = acc[i * heads_dev : (i + 1) * heads_dev].astype(bf16)

    def send_latent(r, where, first):
        slot = my_q * prows + my_z * rows_dev + r

        @pl.loop(first, half)
        def _(i):
            peer = where * half + lax.rem(my_low + i, half)
            k = lax.rem(peer - me + n, n)
            remote(
                lat_send.at[r, peer], lat_recv.at[slot], lat_ss.at[r, k], lat_rs.at[r, k], peer
            ).start()

        if first:
            lat_recv[slot] = lat_send[r, me]

    loads[0].wait()
    for r in range(rows_dev):
        q_rows[r] = q_buf[r].T
    small[0].wait()
    for r in range(rows_dev):
        loads[1 + r].wait()
        if r + 1 < rows_dev:
            loads[2 + r].start()
        if r == 0:
            load_vu.start()
            for copy in small[1:]:
                copy.start()
            for i in range(LOADS):
                w_copy(out_proj, w_sem, i).start()
        attend(r, 1 - side)
        if r == 0:
            pl.semaphore_wait(barrier, n - 1)
        send_latent(r, 1 - side, 0)
    for r in range(rows_dev):
        attend(r, side)
        send_latent(r, side, 1)
    for copy in small[1:]:
        copy.wait()

    lane = lax.broadcasted_iota(jnp.int32, (rows_dev, 128), 1)
    info = jnp.zeros((rows_dev, 128), f32)
    for k in range(ids.shape[1]):
        info = info + jnp.where(lane == ids[:, k : k + 1], weights[:, k : k + 1], 0.0)

    for i in range(chunks):
        gu_copy(gate_proj, g_buf, 0, i).start()
        gu_copy(up_proj, u_buf, 1, i).start()
    load_vu.wait()
    for r in range(rows_dev):

        @pl.loop(1, n)
        def _(k):
            peer = lax.rem(me + n - k, n)
            slot = lax.rem(peer, PLANE) * prows + lax.div(peer, PLANE) * rows_dev + r
            remote(
                lat_send.at[r, peer], lat_recv.at[slot], lat_ss.at[r, k], lat_rs.at[r, k], peer
            ).wait_recv()

    for i in range(rows):
        block = lat_recv[i].astype(f32)
        for j in range(latent // 128):
            lat_f32[j, i * heads_dev : (i + 1) * heads_dev, :] = block[:, j * 128 : (j + 1) * 128]
    for h in range(heads_dev):
        lhs = jnp.concatenate(
            [lat_f32[j, pl.ds(h, rows, stride=heads_dev), :] for j in range(latent // 128)], axis=1
        ).astype(bf16)
        heads[:, h * vdim : (h + 1) * vdim] = jnp.dot(
            lhs, vu_buf[h], preferred_element_type=f32
        ).astype(bf16)

    def stage_a(which, c, lhs, row_scale):
        cols = slice(c * cc, (c + 1) * cc)
        part = jnp.dot(lhs[...], w_buf[:, cols], preferred_element_type=f32)
        if row_scale is not None:
            part = part * row_scale
        for q in range(PLANE):
            piece = part[q * prows : (q + 1) * prows]
            part_f32[c, q] = piece
            a_send[which, c, q] = piece.astype(bf16)
        for k in range(1, PLANE):
            a_copy(which, c, k).start()

    def a_copy(which, c, k):
        return remote(
            a_send.at[which, c, lax.rem(my_q + k, PLANE)],
            a_recv.at[which, c, k - 1],
            a_ss.at[which, c, k - 1],
            a_rs.at[which, c, k - 1],
            plane_peer(k),
        )

    def stage_b(which, c):
        total = part_f32[c, my_q]
        for k in range(1, PLANE):
            a_copy(which, c, k).wait_recv()
            total = total + a_recv[which, c, k - 1].astype(f32)
        for z in range(planes):
            piece = total[z * rows_dev : (z + 1) * rows_dev]
            b_f32[c, z] = piece
            b_send[which, c, z] = piece.astype(bf16)
        for k in range(1, planes):
            b_copy(which, c, k).start()

    def b_copy(which, c, k):
        return remote(
            b_send.at[which, c, lax.rem(my_z + k, planes)],
            b_recv.at[which, c, k - 1],
            b_ss.at[which, c, k - 1],
            b_rs.at[which, c, k - 1],
            z_peer(k),
        )

    def stage_sum(which, c):
        total = b_f32[c, my_z]
        for k in range(1, planes):
            b_copy(which, c, k).wait_recv()
            total = total + b_recv[which, c, k - 1].astype(f32)
        return total

    def z_copy(c, k):
        return remote(
            own_rows.at[c], z_recv.at[c, my_z], z_ss.at[c, k - 1], z_rs.at[c, k - 1], z_peer(k)
        )

    def z_arrival(c, k):
        return remote(
            own_rows.at[c],
            z_recv.at[c, lax.rem(my_z + planes - k, planes)],
            z_ss.at[c, k - 1],
            z_rs.at[c, k - 1],
            z_peer(k),
        )

    def p_copy(c, k):
        return remote(
            p_send.at[c], p_recv.at[c, my_q], p_ss.at[c, k - 1], p_rs.at[c, k - 1], plane_peer(k)
        )

    def p_arrival(c, k):
        return remote(
            p_send.at[c],
            p_recv.at[c, lax.rem(my_q + PLANE - k, PLANE)],
            p_ss.at[c, k - 1],
            p_rs.at[c, k - 1],
            plane_peer(k),
        )

    my_slot = my_q * planes + my_z

    def stage_own(c, square):
        cols = slice(c * cc, (c + 1) * cc)
        value = hidden[:, cols].astype(f32) + stage_sum(0, c)
        residual[c] = value
        scaled = (value * gain[:, cols]).astype(bf16)
        own_rows[c] = scaled
        for k in range(1, planes):
            z_copy(c, k).start()
        z_recv[c, my_z] = scaled
        return square + jnp.sum(value * value, axis=1, keepdims=True)

    def send_info(square):
        inv_rms = lax.rsqrt(square * (1.0 / width) + norm_eps)
        info_own[...] = jnp.where(lane == 127, inv_rms, info)

        @pl.loop(1, n)
        def _(k):
            remote(
                info_own, info_all.at[my_slot], i_ss.at[k], i_rs.at[k], lax.rem(me + k, n)
            ).start()

        info_all[my_slot] = info_own[...]

    def stage_spread(c):
        for k in range(1, planes):
            z_arrival(c, k).wait_recv()
        for z in range(planes):
            p_f32[c, z * rows_dev : (z + 1) * rows_dev, :] = z_recv[c, z].astype(f32)
        block = p_f32[c].astype(bf16)
        p_send[c] = block
        for k in range(1, PLANE):
            p_copy(c, k).start()
        p_recv[c, my_q] = block

    def stage_units(c):
        gu_copy(gate_proj, g_buf, 0, c).wait()
        gu_copy(up_proj, u_buf, 1, c).wait()
        for k in range(1, PLANE):
            p_arrival(c, k).wait_recv()
        x = jnp.concatenate([p_recv[c, q].astype(f32) for q in range(PLANE)], axis=0).astype(bf16)
        span = slice(c * cc, (c + 1) * cc)
        for acc, mat in ((g_acc, g_buf), (u_acc, u_buf)):
            part = jnp.dot(x, mat[span, :], preferred_element_type=f32)
            acc[...] = part if c == 0 else acc[...] + part

    for i in range(LOADS):
        w_copy(out_proj, w_sem, i).wait()
    square = jnp.zeros((rows_dev, 1), f32)
    for stage, c in step_order(chunks, (0.6, 2.4, 3.5, 3.5, 2.4)):
        if stage == 0:
            stage_a(0, c, heads, None)
            if c == chunks - 1:
                for i in range(LOADS):
                    w_copy(down_proj.at[0], d_sem, i).start()
        elif stage == 1:
            stage_b(0, c)
        elif stage == 2:
            square = stage_own(c, square)
            if c == chunks - 1:
                send_info(square)
        elif stage == 3:
            stage_spread(c)
        else:
            stage_units(c)

    @pl.loop(1, n)
    def _(k):
        peer = lax.rem(me + n - k, n)
        slot = lax.rem(peer, PLANE) * planes + lax.div(peer, PLANE)
        remote(info_own, info_all.at[slot], i_ss.at[k], i_rs.at[k], peer).wait_recv()

    for i in range(n):
        info_rows[i * rows_dev : (i + 1) * rows_dev, :] = info_all[i]
    info = info_rows[...]
    lane = lax.broadcasted_iota(jnp.int32, info.shape, 1)
    row_inv = info[:, 127:128]
    row_weight = jnp.sum(jnp.where(lane == me, info, 0.0), axis=1, keepdims=True)
    gate = g_acc[...] * row_inv
    units[...] = (gate / (1.0 + jnp.exp(-gate)) * (u_acc[...] * row_inv)).astype(bf16)
    def drain(which, c):
        for k in range(1, PLANE):
            a_copy(which, c, k).wait_send()
        for k in range(1, planes):
            b_copy(which, c, k).wait_send()

    def drain_first():
        @pl.loop(1, n)
        def _(k):
            peer = lax.rem(me + k, n)
            for r in range(rows_dev):
                remote(
                    lat_send.at[r, peer], lat_recv.at[0], lat_ss.at[r, k], lat_rs.at[r, k], peer
                ).wait_send()
            remote(info_own, info_all.at[0], i_ss.at[k], i_rs.at[k], peer).wait_send()

        for c in range(chunks):
            drain(0, c)
            for k in range(1, planes):
                z_copy(c, k).wait_send()
            for k in range(1, PLANE):
                p_copy(c, k).wait_send()

    for i in range(LOADS):
        w_copy(down_proj.at[0], d_sem, i).wait()
    for stage, c in step_order(chunks, (0.6, 2.4, 3.5)):
        if stage == 0:
            stage_a(1, c, units, row_weight)
            if c == chunks - 1:
                drain_first()
        elif stage == 1:
            stage_b(1, c)
        else:
            out[:, c * cc : (c + 1) * cc] = (residual[c] + stage_sum(1, c)).astype(bf16)

    for c in range(chunks):
        drain(1, c)


def fused_on_device(
    hidden,
    queries,
    latent_cache,
    cache_lengths,
    value_up,
    out_proj,
    norm_gain,
    expert_ids,
    gate_weights,
    gate_proj,
    up_proj,
    down_proj,
):
    n = lax.axis_size("ep")
    planes = n // PLANE
    queries = jnp.swapaxes(queries, 1, 2)
    latent_cache = jnp.swapaxes(latent_cache, 1, 2)
    rows_dev, width = hidden.shape
    rows, prows = n * rows_dev, planes * rows_dev
    heads_dev, latent, vdim = value_up.shape
    ff = gate_proj.shape[2]
    chunks = chunks_of(width)
    cc = width // chunks
    bf16, f32 = jnp.bfloat16, jnp.float32
    vmem, anyspace = pl.BlockSpec(memory_space=pltpu.VMEM), pl.BlockSpec(memory_space=pl.ANY)
    dma = pltpu.SemaphoreType.DMA
    return pl.pallas_call(
        functools.partial(fused_kernel, n),
        out_shape=jax.ShapeDtypeStruct(hidden.shape, bf16),
        in_specs=[anyspace] * 12,
        out_specs=vmem,
        scratch_shapes=[
            pltpu.VMEM(hidden.shape, bf16),
            pltpu.VMEM((1, width), f32),
            pltpu.VMEM(expert_ids.shape, jnp.int32),
            pltpu.VMEM(gate_weights.shape, f32),
            pltpu.SMEM(cache_lengths.shape, jnp.int32),
            pltpu.VMEM((rows_dev, queries.shape[2], queries.shape[1]), bf16),
            pltpu.VMEM(queries.shape, bf16),
            pltpu.VMEM(latent_cache.shape, bf16),
            pltpu.VMEM(value_up.shape, bf16),
            pltpu.VMEM(out_proj.shape, bf16),
            pltpu.VMEM(gate_proj.shape[1:], bf16),
            pltpu.VMEM(up_proj.shape[1:], bf16),
            pltpu.VMEM((rows_dev, n, heads_dev, latent), bf16),
            pltpu.VMEM((rows, heads_dev, latent), bf16),
            pltpu.VMEM((latent // 128, rows * heads_dev, 128), f32),
            pltpu.VMEM((rows, heads_dev * vdim), bf16),
            pltpu.VMEM((chunks, PLANE, prows, cc), f32),
            pltpu.VMEM((2, chunks, PLANE, prows, cc), bf16),
            pltpu.VMEM((2, chunks, PLANE - 1, prows, cc), bf16),
            pltpu.VMEM((chunks, planes, rows_dev, cc), f32),
            pltpu.VMEM((2, chunks, planes, rows_dev, cc), bf16),
            pltpu.VMEM((2, chunks, planes - 1, rows_dev, cc), bf16),
            pltpu.VMEM((chunks, rows_dev, cc), f32),
            pltpu.VMEM((chunks, rows_dev, cc), bf16),
            pltpu.VMEM((chunks, planes, rows_dev, cc), bf16),
            pltpu.VMEM((chunks, prows, cc), f32),
            pltpu.VMEM((chunks, prows, cc), bf16),
            pltpu.VMEM((chunks, PLANE, prows, cc), bf16),
            pltpu.VMEM((rows_dev, 128), f32),
            pltpu.VMEM((n, rows_dev, 128), f32),
            pltpu.VMEM((rows, 128), f32),
            pltpu.VMEM((rows, ff), f32),
            pltpu.VMEM((rows, ff), f32),
            pltpu.VMEM((rows, ff), bf16),
            dma((7 + rows_dev,)),
            dma((LOADS,)),
            dma((2, chunks)),
            dma((LOADS,)),
            dma((rows_dev, n)),
            dma((rows_dev, n)),
            dma((2, chunks, PLANE - 1)),
            dma((2, chunks, PLANE - 1)),
            dma((2, chunks, planes - 1)),
            dma((2, chunks, planes - 1)),
            dma((chunks, planes - 1)),
            dma((chunks, planes - 1)),
            dma((chunks, PLANE - 1)),
            dma((chunks, PLANE - 1)),
            dma((n,)),
            dma((n,)),
        ],
        compiler_params=pltpu.CompilerParams(
            collective_id=0, has_side_effects=True, vmem_limit_bytes=67043328
        ),
        name="fused_layer",
    )(
        hidden,
        queries,
        latent_cache,
        cache_lengths,
        value_up,
        out_proj,
        norm_gain[None, :],
        expert_ids,
        gate_weights,
        gate_proj,
        up_proj,
        down_proj,
    )


def solution(mesh):
    body = fused_on_device if mesh.shape["ep"] == EXPERTS else on_device
    return jax.shard_map(
        body,
        mesh=mesh,
        in_specs=(
            P(("groups", "ep"), None),
            P(("groups", "ep"), None, None),
            P(("groups", "ep"), None, None),
            P(("groups", "ep")),
            P("ep", None, None),
            P("ep", None),
            P(),
            P(("groups", "ep"), None),
            P(("groups", "ep"), None),
            P("ep", None, None),
            P("ep", None, None),
            P("ep", None, None),
        ),
        out_specs=P(("groups", "ep"), None),
        check_vma=False,
    )
```
